32 devices in a mesh: member: 4 (over y, x), region: 8 (over z, core).
Axes of the slice: x: 2, y: 2, z: 4, core: 2. Of those that a mesh axis runs over, the one named last changes fastest.
Arguments:
- states: float32 [256, 49152], P('member', 'region'), may hold values from -6 to 6
- weights: float32 [256, 49152], P('member', 'region'), may hold values from -6 to 6
- obs_count: int32 [384], P('region'), may hold values from 0 to 32
- neighbours: int32 [384, 12], P('region'), may hold values from 0 to 383, as said below
Outputs:
- increments: float32 [256, 49152], P('member', 'region')
The draws below stay inside these ranges and needn't reach their ends.
Inputs may be any that keep to these rules, and one draw needn't show every extreme that they name: `neighbours`: each row lists 12 distinct tiles, all within 8 tiles of its own tile counting cyclically over the 384 tiles; the list always holds the tile itself and the tiles exactly 8 before and after it, in a drawn order.
All inputs are finite; a program needn't handle non-finite values.
Results may differ from the reference program's by a relative error of at most 0.0003.
Values sent between devices are 32-bit elements; how exact they have to be, the bound alone decides.
A program may use at most 128 MiB of HBM per device.

```python
import jax
import jax.numpy as jnp
from jax import lax

M = 256
TILE = 128
NEIGHBOURS = 12
HALO_TILES = 8
TPD = 12
TILES = 384
ROWS = 49152


def draw_neighbours(key, part):
    spread = jnp.concatenate([jnp.arange(-HALO_TILES + 1, 0, dtype=jnp.int32), jnp.arange(1, HALO_TILES, dtype=jnp.int32)])
    fixed_part = jnp.array([0, -HALO_TILES, HALO_TILES], dtype=jnp.int32)
    picks = NEIGHBOURS - 3
    keys = jax.random.split(jax.random.fold_in(key, 7), TILES)

    def one_tile(tile_key):
        first_key, second_key = jax.random.split(tile_key)
        chosen = spread[jax.random.permutation(first_key, spread.shape[0])[:picks]]
        offsets = jnp.concatenate([fixed_part, chosen])
        return offsets[jax.random.permutation(second_key, NEIGHBOURS)]
    offsets = jax.vmap(one_tile)(keys)
    tiles_here = jnp.arange(TILES, dtype=jnp.int32)[:, None]
    return ((tiles_here + offsets) % TILES).astype(jnp.int32)


def place_ends(values, key, low, high):
    spot = [jax.random.randint(jax.random.fold_in(key, axis), (), 0, length) for axis, length in enumerate(values.shape)]
    longest = values.shape.index(max(values.shape))
    next_to = spot[:longest] + [(spot[longest] + 1) % values.shape[longest]] + spot[longest + 1:]
    return values.at[tuple(spot)].set(low).at[tuple(next_to)].set(high)


def level_of(own_key, dims, shards, low, top_value):
    loudness, own = 1.0, jax.random.fold_in(own_key, 6)
    for dim, shards_of in shards:
        steps = jnp.exp(jax.random.uniform(jax.random.fold_in(own, dim), (shards_of,), jnp.float32, low / len(shards), top_value / len(shards)))
        loudness = loudness * jnp.repeat(steps, dims[dim] // shards_of).reshape([-1 if axis == dim else 1 for axis in range(len(dims))])
    return loudness


def bell_draw(stream_key, extent, deviation, reach, cuts=(), kind=jnp.bfloat16):
    loudness = level_of(stream_key, extent, cuts, -0.22, 0.18) if cuts else 1.0
    drawn = jax.random.normal(stream_key, extent, jnp.float32) * deviation * loudness
    return jnp.minimum(jnp.maximum(drawn, -reach), reach).astype(kind)


def setup_inputs(seed: int = 0) -> dict:
    splits = jax.random.split(jax.random.key(seed), 5)
    states = bell_draw(splits[0], (M, ROWS), 1.0, 6.0, ((0, 4), (1, 8)), jnp.float32)
    weights = bell_draw(splits[1], (M, ROWS), 1.0, 6.0, ((0, 4), (1, 8)), jnp.float32)
    obs_count = place_ends(jax.random.randint(splits[2], (TILES,), 0, 33), jax.random.fold_in(splits[2], 1), 0, 32).astype(jnp.int32)
    neighbours = draw_neighbours(jax.random.fold_in(splits[4], 71), 0)
    return {"states": states, "weights": weights, "obs_count": obs_count, "neighbours": neighbours}


def taper(offset, tile):
    rows = jnp.arange(tile, dtype=jnp.float32)
    spread = tile * offset[:, None, None] + rows[None, None, :] - rows[None, :, None]
    scaled = spread / (2.0 * tile)
    return 1.0 / (1.0 + scaled * scaled)


def reference(states, weights, obs_count, neighbours):
    members = states.shape[0]
    counts = obs_count.astype(jnp.float32)
    factor = counts / (counts + 8.0)
    state_rows = states.T
    weight_rows = weights.T
    anomaly = state_rows - jnp.mean(state_rows, axis=1, keepdims=True)
    scaled = weight_rows.reshape(TILES, TILE, members) * factor[:, None, None]
    blocks = anomaly.reshape(TILES, TILE, members)

    def group(first):
        own = first + jnp.arange(TPD, dtype=jnp.int32)
        mine = lax.dynamic_slice_in_dim(blocks, first, TPD, 0)
        lists = lax.dynamic_slice_in_dim(neighbours, first, TPD, 0)
        total = jnp.zeros((TPD, TILE, members), jnp.float32)
        for slot in range(NEIGHBOURS):
            chosen = lists[:, slot].astype(jnp.int32)
            offset = ((chosen - own + TILES // 2) % TILES - TILES // 2).astype(jnp.float32)
            others = blocks[chosen]
            other_weights = scaled[chosen]
            covar = jnp.einsum("tim,tjm->tij", mine, others, precision=lax.Precision.HIGHEST) / (members - 1.0)
            total = total + jnp.einsum("tij,tjm->tim", taper(offset, TILE) * covar, other_weights, precision=lax.Precision.HIGHEST)
        return total

    starts = jnp.arange(TILES // TPD, dtype=jnp.int32) * TPD
    result = lax.map(group, starts)
    return result.reshape(ROWS, members).T
```

```python
import jax
import jax.numpy as jnp
from jax import lax
from jax.experimental import pallas as pl
from jax.experimental.pallas import tpu as pltpu
from jax.sharding import PartitionSpec as P

TILE = 128
HALO_TILES = 8
TPD = 12


def extended_2(block, sides, width):
    for axis, dim in sides:
        count = lax.axis_size(axis)
        forward = [(i, i + 1) for i in range(count - 1)]
        forward.append((count - 1, 0))
        backward = [(target, source) for source, target in forward]
        low = lax.ppermute(
            lax.slice_in_dim(block, block.shape[dim] - width, None, axis=dim), axis, forward
        )
        high = lax.ppermute(lax.slice_in_dim(block, 0, width, axis=dim), axis, backward)
        block = jnp.concatenate([low, block, high], axis=dim)
    return block


def taper(offset, tile):
    rows = jnp.arange(tile, dtype=jnp.float32)
    spread = tile * offset[:, None, None] + rows[None, None, :] - rows[None, :, None]
    scaled = spread / (2.0 * tile)
    return 1.0 / (1.0 + scaled * scaled)


def shards(states, weights, obs_count, neighbours):
    member_count = lax.axis_size("member")
    region_count = lax.axis_size("region")
    member_part, local_rows = states.shape
    local_tiles = local_rows // TILE
    counts = obs_count.astype(jnp.float32)
    factor = counts / (counts + 8.0)
    scaled = (weights.reshape(member_part, local_tiles, TILE) * factor[None, :, None]).reshape(
        member_part, local_rows
    )
    stacked = jnp.stack([states, scaled])
    rim = HALO_TILES * TILE
    block = TPD * TILE
    padded = extended_2(stacked, (("region", 2),), rim)
    own_block = lax.all_to_all(stacked, "member", split_axis=2, concat_axis=1, tiled=True)
    extended = extended_2(own_block, (("member", 2),), rim)
    below, above = (
        lax.all_gather(padded[:, :, :rim], "member", axis=1, tiled=True),
        lax.all_gather(padded[:, :, rim + local_rows :], "member", axis=1, tiled=True),
    )
    position = lax.axis_index("member")
    lower = jnp.where(position == 0, below, extended[:, :, :rim])
    upper = jnp.where(position == member_count - 1, above, extended[:, :, rim + block :])
    window = jnp.concatenate([lower, extended[:, :, rim : rim + block], upper], axis=2)
    members = window.shape[1]
    anomaly = window[0] - jnp.mean(window[0], axis=0, keepdims=True)
    window_weights = window[1]
    tiles_all = TPD * member_count * region_count
    first_tile = (lax.axis_index("region") * member_count + lax.axis_index("member")) * TPD
    lists = lax.dynamic_slice_in_dim(neighbours, lax.axis_index("member") * TPD, TPD, 0)
    local_ids = (lists - first_tile + HALO_TILES) % tiles_all
    span_count = 2 * HALO_TILES + 1
    tile_places = jnp.arange(TPD, dtype=jnp.int32)
    shift_places = jnp.arange(span_count, dtype=jnp.int32)
    wanted = tile_places[:, None, None] + shift_places[None, None, :]
    keep_table = jnp.sum((local_ids[:, :, None] == wanted).astype(jnp.float32), axis=1)
    mine = anomaly[:, rim : rim + block].reshape(members, TPD, TILE)

    def add_offset(shift, total):
        others = lax.dynamic_slice_in_dim(anomaly, shift * TILE, block, 1).reshape(
            members, TPD, TILE
        )
        other_weights = lax.dynamic_slice_in_dim(window_weights, shift * TILE, block, 1).reshape(
            members, TPD, TILE
        )
        covar = jnp.einsum("mti,mtj->tij", mine, others, precision=lax.Precision.HIGHEST) / (
            members - 1.0
        )
        offset = jnp.full((TPD,), shift - HALO_TILES).astype(jnp.float32)
        keep = lax.dynamic_index_in_dim(keep_table, shift, 1, keepdims=False)
        coefficient = taper(offset, TILE) * covar * keep[:, None, None]
        return total + jnp.einsum(
            "mtj,tij->mti", other_weights, coefficient, precision=lax.Precision.HIGHEST
        )

    total = lax.fori_loop(0, span_count, add_offset, jnp.zeros((members, TPD, TILE), jnp.float32))
    returned = lax.all_to_all(
        total.reshape(members, block), "member", split_axis=0, concat_axis=1, tiled=True
    )
    return returned


BLOCK = 2 * TILE
SPAN = HALO_TILES + 1
RIM = HALO_TILES * TILE


def split(value):
    high = value.astype(jnp.bfloat16)
    return high, (value - high.astype(jnp.float32)).astype(jnp.bfloat16)


def dot(left, right):
    return jnp.dot(left, right, preferred_element_type=jnp.float32)


def fill_taper(taper_ref, members):
    rows = lax.broadcasted_iota(jnp.int32, (BLOCK, BLOCK), 0)
    columns = lax.broadcasted_iota(jnp.int32, (BLOCK, BLOCK), 1)
    for k in range(SPAN):
        spread = (columns - rows + (2 * k - HALO_TILES) * TILE).astype(jnp.float32) / (2.0 * TILE)
        taper_ref[k] = 1.0 / ((1.0 + spread * spread) * (members - 1.0))


def prepare_states(value, block, own, low_ref, high_ref, low_t_ref, high_t_ref):
    anomaly = value - jnp.mean(value, axis=0, keepdims=True)
    high_ref[block], low_ref[block] = split(anomaly)
    if own is not None:
        high_t_ref[own], low_t_ref[own] = split(anomaly.T)


def prepare_weights(value, block, weight_ref):
    high = value.astype(jnp.bfloat16).astype(jnp.float32)
    weight_ref[block] = jnp.concatenate([high, value - high], axis=0).T.astype(jnp.bfloat16)


def pair_increment(pair, keep_ref, low_ref, high_ref, low_t_ref, high_t_ref, weight_ref, taper_ref):
    total = None
    for k in range(SPAN):
        left_high, left_low = high_t_ref[pair], low_t_ref[pair]
        right_high, right_low = high_ref[pair + k], low_ref[pair + k]
        covar = dot(left_high, right_high) + dot(left_low, right_high) + dot(left_high, right_low)
        scaled = covar * taper_ref[k]
        rows = []
        for s in range(2):
            rows.append(
                jnp.concatenate(
                    [
                        scaled[s * TILE : (s + 1) * TILE, t * TILE : (t + 1) * TILE]
                        * keep_ref[2 * pair + s, 2 * k + t + 1 - s]
                        for t in range(2)
                    ],
                    axis=1,
                )
            )
        high, low = split(jnp.concatenate(rows, axis=0))
        weight = weight_ref[pair + k]
        term = dot(high, weight) + dot(low, weight)
        total = term if total is None else total + term
    half = total.shape[1] // 2
    return (total[:, :half] + total[:, half:]).T


def local_kernel(states_ref, weights_ref, keep_ref, out_ref, low_ref, high_ref, low_t_ref, high_t_ref, weight_ref, taper_ref):
    members, window = states_ref.shape
    blocks = window // BLOCK
    rim = RIM // BLOCK
    pairs = blocks - 2 * rim
    fill_taper(taper_ref, members)

    def prepare(block, own):
        columns = pl.ds(pl.multiple_of(block * BLOCK, BLOCK), BLOCK)
        prepare_states(states_ref[:, columns], block, own, low_ref, high_ref, low_t_ref, high_t_ref)
        prepare_weights(weights_ref[:, columns], block, weight_ref)

    pl.loop(0, rim)(lambda b: prepare(b, None))
    pl.loop(0, pairs)(lambda b: prepare(b + rim, b))
    pl.loop(0, rim)(lambda b: prepare(b + rim + pairs, None))

    @pl.loop(0, pairs)
    def _(pair):
        columns = pl.ds(pl.multiple_of(pair * BLOCK, BLOCK), BLOCK)
        out_ref[:, columns] = pair_increment(
            pair, keep_ref, low_ref, high_ref, low_t_ref, high_t_ref, weight_ref, taper_ref
        )


def scratch_of(members, part, pairs):
    rim = RIM // BLOCK
    blocks = pairs + 2 * rim
    bf16 = jnp.bfloat16
    return [
        pltpu.VMEM((blocks, members, BLOCK), bf16),
        pltpu.VMEM((blocks, members, BLOCK), bf16),
        pltpu.VMEM((pairs, BLOCK, members), bf16),
        pltpu.VMEM((pairs, BLOCK, members), bf16),
        pltpu.VMEM((blocks, BLOCK, 2 * part), bf16),
        pltpu.VMEM((SPAN, BLOCK, BLOCK), jnp.float32),
    ]


def keep_table_of(neighbours, factor_window, tiles_all):
    local_tiles = neighbours.shape[0]
    first = lax.axis_index("region") * local_tiles
    own = first + jnp.arange(local_tiles, dtype=jnp.int32)
    shift = (neighbours - own[:, None] + HALO_TILES + 1) % tiles_all
    places = jnp.arange(2 * SPAN + 2, dtype=jnp.int32)
    return jnp.sum((shift[:, :, None] == places).astype(jnp.float32), axis=1)


def local_increment(states, weights, keep):
    members, window = states.shape
    part = weights.shape[0]
    pairs = window // BLOCK - 2 * (RIM // BLOCK)
    vmem = pl.BlockSpec(memory_space=pltpu.VMEM)
    return pl.pallas_call(
        local_kernel,
        out_shape=jax.ShapeDtypeStruct((part, pairs * BLOCK), jnp.float32),
        in_specs=[vmem, vmem, pl.BlockSpec(memory_space=pltpu.SMEM)],
        out_specs=vmem,
        scratch_shapes=scratch_of(members, part, pairs),
        compiler_params=pltpu.CompilerParams(vmem_limit_bytes=60 * 1024 * 1024),
    )(states, weights, keep)


def region_shards(states, weights, obs_count, neighbours):
    region_count = lax.axis_size("region")
    part, local_rows = states.shape
    counts = obs_count.astype(jnp.float32)
    factor = counts / (counts + 8.0)
    scaled = (weights.reshape(part, local_rows // TILE, TILE) * factor[None, :, None]).reshape(part, local_rows)
    gathered = lax.all_gather(states, "member", axis=0, tiled=True)
    window = extended_2(gathered, (("region", 1),), RIM)
    weight_window = extended_2(scaled, (("region", 1),), RIM)
    keep = keep_table_of(neighbours, None, region_count * (local_rows // TILE))
    return local_increment(window, weight_window, keep)


def fits(states, weights, obs_count, neighbours):
    part, local_rows = states.shape
    members = part * lax.axis_size("member")
    window = local_rows + 2 * RIM
    return (
        local_rows % RIM == 0
        and local_rows >= RIM
        and members % 128 == 0
        and part % 64 == 0
        and window * (members * 12 + part * 16) <= 46 * 1024 * 1024
    )


def either(*arguments):
    return region_shards(*arguments) if fits(*arguments) else shards(*arguments)


def solution(mesh):
    placed = (P("member", "region"), P("member", "region"), P("region"), P("region", None))
    return jax.shard_map(
        either, mesh=mesh, in_specs=placed, out_specs=P("member", "region"), check_vma=False
    )
```

```python
import jax
import jax.numpy as jnp
from jax import lax
from jax.experimental import pallas as pl
from jax.experimental.pallas import tpu as pltpu
from jax.sharding import PartitionSpec as P

TILE = 128
HALO_TILES = 8
TPD = 12


def extended_2(block, sides, width):
    for axis, dim in sides:
        count = lax.axis_size(axis)
        forward = [(i, i + 1) for i in range(count - 1)]
        forward.append((count - 1, 0))
        backward = [(target, source) for source, target in forward]
        low = lax.ppermute(
            lax.slice_in_dim(block, block.shape[dim] - width, None, axis=dim), axis, forward
        )
        high = lax.ppermute(lax.slice_in_dim(block, 0, width, axis=dim), axis, backward)
        block = jnp.concatenate([low, block, high], axis=dim)
    return block


def taper(offset, tile):
    rows = jnp.arange(tile, dtype=jnp.float32)
    spread = tile * offset[:, None, None] + rows[None, None, :] - rows[None, :, None]
    scaled = spread / (2.0 * tile)
    return 1.0 / (1.0 + scaled * scaled)


def shards(states, weights, obs_count, neighbours):
    member_count = lax.axis_size("member")
    region_count = lax.axis_size("region")
    member_part, local_rows = states.shape
    local_tiles = local_rows // TILE
    counts = obs_count.astype(jnp.float32)
    factor = counts / (counts + 8.0)
    scaled = (weights.reshape(member_part, local_tiles, TILE) * factor[None, :, None]).reshape(
        member_part, local_rows
    )
    stacked = jnp.stack([states, scaled])
    rim = HALO_TILES * TILE
    block = TPD * TILE
    padded = extended_2(stacked, (("region", 2),), rim)
    own_block = lax.all_to_all(stacked, "member", split_axis=2, concat_axis=1, tiled=True)
    extended = extended_2(own_block, (("member", 2),), rim)
    below, above = (
        lax.all_gather(padded[:, :, :rim], "member", axis=1, tiled=True),
        lax.all_gather(padded[:, :, rim + local_rows :], "member", axis=1, tiled=True),
    )
    position = lax.axis_index("member")
    lower = jnp.where(position == 0, below, extended[:, :, :rim])
    upper = jnp.where(position == member_count - 1, above, extended[:, :, rim + block :])
    window = jnp.concatenate([lower, extended[:, :, rim : rim + block], upper], axis=2)
    members = window.shape[1]
    anomaly = window[0] - jnp.mean(window[0], axis=0, keepdims=True)
    window_weights = window[1]
    tiles_all = TPD * member_count * region_count
    first_tile = (lax.axis_index("region") * member_count + lax.axis_index("member")) * TPD
    lists = lax.dynamic_slice_in_dim(neighbours, lax.axis_index("member") * TPD, TPD, 0)
    local_ids = (lists - first_tile + HALO_TILES) % tiles_all
    span_count = 2 * HALO_TILES + 1
    tile_places = jnp.arange(TPD, dtype=jnp.int32)
    shift_places = jnp.arange(span_count, dtype=jnp.int32)
    wanted = tile_places[:, None, None] + shift_places[None, None, :]
    keep_table = jnp.sum((local_ids[:, :, None] == wanted).astype(jnp.float32), axis=1)
    mine = anomaly[:, rim : rim + block].reshape(members, TPD, TILE)

    def add_offset(shift, total):
        others = lax.dynamic_slice_in_dim(anomaly, shift * TILE, block, 1).reshape(
            members, TPD, TILE
        )
        other_weights = lax.dynamic_slice_in_dim(window_weights, shift * TILE, block, 1).reshape(
            members, TPD, TILE
        )
        covar = jnp.einsum("mti,mtj->tij", mine, others, precision=lax.Precision.HIGHEST) / (
            members - 1.0
        )
        offset = jnp.full((TPD,), shift - HALO_TILES).astype(jnp.float32)
        keep = lax.dynamic_index_in_dim(keep_table, shift, 1, keepdims=False)
        coefficient = taper(offset, TILE) * covar * keep[:, None, None]
        return total + jnp.einsum(
            "mtj,tij->mti", other_weights, coefficient, precision=lax.Precision.HIGHEST
        )

    total = lax.fori_loop(0, span_count, add_offset, jnp.zeros((members, TPD, TILE), jnp.float32))
    returned = lax.all_to_all(
        total.reshape(members, block), "member", split_axis=0, concat_axis=1, tiled=True
    )
    return returned


BLOCK = 2 * TILE
SPAN = HALO_TILES + 1
RIM = HALO_TILES * TILE


def split(value):
    high = value.astype(jnp.bfloat16)
    return high, (value - high.astype(jnp.float32)).astype(jnp.bfloat16)


def dot(left, right):
    return jnp.dot(left, right, preferred_element_type=jnp.float32)


def fill_taper(taper_ref, members):
    rows = lax.broadcasted_iota(jnp.int32, (BLOCK, BLOCK), 0)
    columns = lax.broadcasted_iota(jnp.int32, (BLOCK, BLOCK), 1)
    for k in range(SPAN):
        spread = (columns - rows + (2 * k - HALO_TILES) * TILE).astype(jnp.float32) / (2.0 * TILE)
        taper_ref[k] = 1.0 / ((1.0 + spread * spread) * (members - 1.0))


def prepare_states(value, block, own, low_ref, high_ref, low_t_ref, high_t_ref):
    anomaly = value - jnp.mean(value, axis=0, keepdims=True)
    high_ref[block], low_ref[block] = split(anomaly)
    if own is not None:
        high_t_ref[own], low_t_ref[own] = split(anomaly.T)


def prepare_weights(value, block, weight_ref):
    high = value.astype(jnp.bfloat16).astype(jnp.float32)
    weight_ref[block] = jnp.concatenate([high, value - high], axis=0).T.astype(jnp.bfloat16)


def pair_rows(pair, keep_ref, low_ref, high_ref, low_t_ref, high_t_ref, taper_ref, x_high_ref, x_low_ref):
    for k in range(SPAN):
        left_high, left_low = high_t_ref[pair], low_t_ref[pair]
        right_high, right_low = high_ref[pair + k], low_ref[pair + k]
        covar = dot(left_high, right_high) + dot(left_low, right_high) + dot(left_high, right_low)
        scaled = covar * taper_ref[k]
        for s in range(2):
            for t in range(2):
                rows, columns = slice(s * TILE, (s + 1) * TILE), slice(t * TILE, (t + 1) * TILE)
                value = scaled[rows, columns] * keep_ref[2 * pair + s, 2 * k + t + 1 - s]
                place = slice((2 * k + t) * TILE, (2 * k + t + 1) * TILE)
                x_high_ref[rows, place], x_low_ref[rows, place] = split(value)


def pair_apply(pair, weight_ref, x_high_ref, x_low_ref):
    weight = weight_ref[pl.ds(pair, SPAN)].reshape(SPAN * BLOCK, weight_ref.shape[2])
    total = dot(x_high_ref[...], weight) + dot(x_low_ref[...], weight)
    half = total.shape[1] // 2
    return (total[:, :half] + total[:, half:]).T


def scratch_of(members, part, pairs):
    rim = RIM // BLOCK
    blocks = pairs + 2 * rim
    bf16 = jnp.bfloat16
    return [
        pltpu.VMEM((blocks, members, BLOCK), bf16),
        pltpu.VMEM((blocks, members, BLOCK), bf16),
        pltpu.VMEM((pairs, BLOCK, members), bf16),
        pltpu.VMEM((pairs, BLOCK, members), bf16),
        pltpu.VMEM((blocks, BLOCK, 2 * part), bf16),
        pltpu.VMEM((SPAN, BLOCK, BLOCK), jnp.float32),
    ] + [pltpu.VMEM((BLOCK, SPAN * BLOCK), bf16)] * 4


def keep_table_of(neighbours, factor_window, tiles_all):
    local_tiles = neighbours.shape[0]
    first = lax.axis_index("region") * local_tiles
    own = first + jnp.arange(local_tiles, dtype=jnp.int32)
    shift = (neighbours - own[:, None] + HALO_TILES + 1) % tiles_all
    places = jnp.arange(2 * SPAN + 2, dtype=jnp.int32)
    return jnp.sum((shift[:, :, None] == places).astype(jnp.float32), axis=1)


def region_kernel(
    own_ref, weights_ref, factor_ref, keep_ref, out_ref,
    low_ref, high_ref, low_t_ref, high_t_ref, weight_ref, taper_ref, xh0, xl0, xh1, xl1,
    held, weight_rim, factor_rim,
    direct_send, direct_recv, relay_send, relay_recv, rim_send, rim_recv,
):
    part, rows = own_ref.shape
    count = rows // RIM
    per_chunk = RIM // BLOCK
    half = part // 2
    member, region = lax.axis_index("member"), lax.axis_index("region")
    regions = lax.axis_size("region")
    beside = member + 1 - 2 * lax.rem(member, 2)
    across = lax.rem(member + 2, 4)
    partners = ((beside, region), (across, region))
    above = (member, lax.rem(region + 1, regions))
    below = (member, lax.rem(region + regions - 1, regions))

    barrier = pltpu.get_barrier_semaphore()
    for device in partners + (above, below):
        pl.semaphore_signal(barrier, inc=1, device_id=device, device_id_type=pl.DeviceIdType.MESH)
    pl.semaphore_wait(barrier, 4)

    def chunk_at(step):
        return jnp.where(step == 0, count, step)

    def copy(source, target, send, recv, device):
        return pltpu.make_async_remote_copy(
            src_ref=source, dst_ref=target, send_sem=send, recv_sem=recv,
            device_id=device, device_id_type=pl.DeviceIdType.MESH,
        )

    def columns_of(chunk):
        return pl.ds(pl.multiple_of((chunk - 1) * RIM, RIM), RIM)

    def direct(step, side):
        chunk = chunk_at(step)
        return copy(
            own_ref.at[:, columns_of(chunk)], held.at[chunk, 1 + side],
            direct_send.at[side, step], direct_recv.at[side, step], partners[side],
        )

    def relay(step, side):
        chunk = chunk_at(step)
        strip = pl.ds(side * half, half)
        return copy(
            held.at[chunk, 2 - side, strip], held.at[chunk, 3, strip],
            relay_send.at[side, step], relay_recv.at[side, step], partners[side],
        )

    def rim(up, item):
        device = above if up else below
        edge, place = (count, 0) if up else (1, count + 1)
        spot = 0 if up else 1
        columns = slice((edge - 1) * RIM, edge * RIM)
        if item == 4:
            source, target = weights_ref.at[:, columns], weight_rim.at[spot]
        elif item == 5:
            source, target = factor_ref.at[:, columns], factor_rim.at[spot]
        elif item == 0:
            source, target = own_ref.at[:, columns], held.at[place, 0]
        else:
            source, target = held.at[edge, item], held.at[place, item]
        return copy(source, target, rim_send.at[spot, item], rim_recv.at[spot, item], device)

    for step in range(2):
        for side in range(2):
            direct(step, side).start()
    for item in (0, 4, 5):
        for up in (True, False):
            rim(up, item).start()

    fill_taper(taper_ref, part * 4)

    @pl.loop(0, count * per_chunk)
    def _(block):
        columns = pl.ds(pl.multiple_of(block * BLOCK, BLOCK), BLOCK)
        prepare_weights(weights_ref[:, columns] * factor_ref[0:1, columns], block + per_chunk, weight_ref)

    def prepare_own(chunk):
        @pl.loop(0, per_chunk)
        def _(b):
            block = (chunk - 1) * per_chunk + b
            inner = pl.ds(pl.multiple_of(b * BLOCK, BLOCK), BLOCK)
            mine = own_ref[:, pl.ds(pl.multiple_of(block * BLOCK, BLOCK), BLOCK)]
            value = jnp.concatenate([mine] + [held[chunk, slot, :, inner] for slot in range(1, 4)], axis=0)
            prepare_states(value, block + per_chunk, block, low_ref, high_ref, low_t_ref, high_t_ref)

    def prepare_rim(up):
        place, spot = (0, 0) if up else (count + 1, 1)

        @pl.loop(0, per_chunk)
        def _(b):
            inner = pl.ds(pl.multiple_of(b * BLOCK, BLOCK), BLOCK)
            value = jnp.concatenate([held[place, slot, :, inner] for slot in range(4)], axis=0)
            block = place * per_chunk + b
            prepare_states(value, block, None, low_ref, high_ref, low_t_ref, high_t_ref)
            prepare_weights(weight_rim[spot, :, inner] * factor_rim[spot, 0:1, inner], block, weight_ref)

    @pl.loop(0, count + 3)
    def _(step):
        @pl.when(step < count)
        def _():
            for side in range(2):
                direct(step, side).wait_recv()
            for side in range(2):
                relay(step, side).start()

        @pl.when(step + 2 < count)
        def _():
            for side in range(2):
                direct(step + 2, side).start()

        for first, up in ((0, True), (1, False)):
            @pl.when(step == first)
            def _():
                for item in (1, 2):
                    rim(up, item).start()

        @pl.when((step >= 1) & (step <= count))
        def _():
            for side in range(2):
                relay(step - 1, side).wait_recv()

        for first, up in ((1, True), (2, False)):
            @pl.when(step == first)
            def _():
                rim(up, 3).start()

        @pl.when((step >= 1) & (step <= count))
        def _():
            prepare_own(chunk_at(step - 1))

        for first, up in ((3, True), (4, False)):
            @pl.when(step == first)
            def _():
                for item in range(6):
                    rim(up, item).wait_recv()
                prepare_rim(up)

        @pl.when(step >= 3)
        def _():
            @pl.loop(0, per_chunk // 2)
            def _(b):
                pair = (step - 3) * per_chunk + 2 * b
                pair_rows(pair, keep_ref, low_ref, high_ref, low_t_ref, high_t_ref, taper_ref, xh0, xl0)
                pair_rows(pair + 1, keep_ref, low_ref, high_ref, low_t_ref, high_t_ref, taper_ref, xh1, xl1)
                columns = pl.ds(pl.multiple_of(pair * BLOCK, BLOCK), BLOCK)
                out_ref[:, columns] = pair_apply(pair, weight_ref, xh0, xl0)
                after = pl.ds(pl.multiple_of((pair + 1) * BLOCK, BLOCK), BLOCK)
                out_ref[:, after] = pair_apply(pair + 1, weight_ref, xh1, xl1)

    @pl.loop(0, count)
    def _(step):
        for side in range(2):
            direct(step, side).wait_send()
            relay(step, side).wait_send()

    for up in (True, False):
        for item in range(6):
            rim(up, item).wait_send()


def region_shards(states, weights, obs_count, neighbours):
    region_count = lax.axis_size("region")
    part, local_rows = states.shape
    members = part * lax.axis_size("member")
    count = local_rows // RIM
    pairs = local_rows // BLOCK
    counts = obs_count.astype(jnp.float32)
    factor = counts / (counts + 8.0)
    factor_rows = jnp.broadcast_to(factor[None, :, None], (8, local_rows // TILE, TILE)).reshape(8, local_rows)
    keep = keep_table_of(neighbours, None, region_count * (local_rows // TILE))
    vmem = pl.BlockSpec(memory_space=pltpu.VMEM)
    dma = pltpu.SemaphoreType.DMA
    return pl.pallas_call(
        region_kernel,
        out_shape=jax.ShapeDtypeStruct((part, local_rows), jnp.float32),
        in_specs=[vmem, vmem, vmem, pl.BlockSpec(memory_space=pltpu.SMEM)],
        out_specs=vmem,
        scratch_shapes=scratch_of(members, part, pairs)
        + [
            pltpu.VMEM((count + 2, 4, part, RIM), jnp.float32),
            pltpu.VMEM((2, part, RIM), jnp.float32),
            pltpu.VMEM((2, 8, RIM), jnp.float32),
            dma((2, count)), dma((2, count)), dma((2, count)), dma((2, count)),
            dma((2, 6)), dma((2, 6)),
        ],
        compiler_params=pltpu.CompilerParams(
            collective_id=0, has_side_effects=True, vmem_limit_bytes=60 * 1024 * 1024
        ),
    )(states, weights, factor_rows, keep)


def fits(states, weights, obs_count, neighbours):
    part, local_rows = states.shape
    members = part * lax.axis_size("member")
    window = local_rows + 2 * RIM
    return (
        lax.axis_size("member") == 4
        and lax.axis_size("region") > 2
        and local_rows % RIM == 0
        and local_rows >= 3 * RIM
        and members % 128 == 0
        and part % 64 == 0
        and window * (members * 12 + part * 16) <= 46 * 1024 * 1024
    )


def either(*arguments):
    return region_shards(*arguments) if fits(*arguments) else shards(*arguments)


def solution(mesh):
    placed = (P("member", "region"), P("member", "region"), P("region"), P("region", None))
    return jax.shard_map(
        either, mesh=mesh, in_specs=placed, out_specs=P("member", "region"), check_vma=False
    )
```

```python
import jax
import jax.numpy as jnp
from jax import lax
from jax.experimental import pallas as pl
from jax.experimental.pallas import tpu as pltpu
from jax.sharding import PartitionSpec as P

TILE = 128
HALO_TILES = 8
TPD = 12


def extended_2(block, sides, width):
    for axis, dim in sides:
        count = lax.axis_size(axis)
        forward = [(i, i + 1) for i in range(count - 1)]
        forward.append((count - 1, 0))
        backward = [(target, source) for source, target in forward]
        low = lax.ppermute(
            lax.slice_in_dim(block, block.shape[dim] - width, None, axis=dim), axis, forward
        )
        high = lax.ppermute(lax.slice_in_dim(block, 0, width, axis=dim), axis, backward)
        block = jnp.concatenate([low, block, high], axis=dim)
    return block


def taper(offset, tile):
    rows = jnp.arange(tile, dtype=jnp.float32)
    spread = tile * offset[:, None, None] + rows[None, None, :] - rows[None, :, None]
    scaled = spread / (2.0 * tile)
    return 1.0 / (1.0 + scaled * scaled)


def shards(states, weights, obs_count, neighbours):
    member_count = lax.axis_size("member")
    region_count = lax.axis_size("region")
    member_part, local_rows = states.shape
    local_tiles = local_rows // TILE
    counts = obs_count.astype(jnp.float32)
    factor = counts / (counts + 8.0)
    scaled = (weights.reshape(member_part, local_tiles, TILE) * factor[None, :, None]).reshape(
        member_part, local_rows
    )
    stacked = jnp.stack([states, scaled])
    rim = HALO_TILES * TILE
    block = TPD * TILE
    padded = extended_2(stacked, (("region", 2),), rim)
    own_block = lax.all_to_all(stacked, "member", split_axis=2, concat_axis=1, tiled=True)
    extended = extended_2(own_block, (("member", 2),), rim)
    below, above = (
        lax.all_gather(padded[:, :, :rim], "member", axis=1, tiled=True),
        lax.all_gather(padded[:, :, rim + local_rows :], "member", axis=1, tiled=True),
    )
    position = lax.axis_index("member")
    lower = jnp.where(position == 0, below, extended[:, :, :rim])
    upper = jnp.where(position == member_count - 1, above, extended[:, :, rim + block :])
    window = jnp.concatenate([lower, extended[:, :, rim : rim + block], upper], axis=2)
    members = window.shape[1]
    anomaly = window[0] - jnp.mean(window[0], axis=0, keepdims=True)
    window_weights = window[1]
    tiles_all = TPD * member_count * region_count
    first_tile = (lax.axis_index("region") * member_count + lax.axis_index("member")) * TPD
    lists = lax.dynamic_slice_in_dim(neighbours, lax.axis_index("member") * TPD, TPD, 0)
    local_ids = (lists - first_tile + HALO_TILES) % tiles_all
    span_count = 2 * HALO_TILES + 1
    tile_places = jnp.arange(TPD, dtype=jnp.int32)
    shift_places = jnp.arange(span_count, dtype=jnp.int32)
    wanted = tile_places[:, None, None] + shift_places[None, None, :]
    keep_table = jnp.sum((local_ids[:, :, None] == wanted).astype(jnp.float32), axis=1)
    mine = anomaly[:, rim : rim + block].reshape(members, TPD, TILE)

    def add_offset(shift, total):
        others = lax.dynamic_slice_in_dim(anomaly, shift * TILE, block, 1).reshape(
            members, TPD, TILE
        )
        other_weights = lax.dynamic_slice_in_dim(window_weights, shift * TILE, block, 1).reshape(
            members, TPD, TILE
        )
        covar = jnp.einsum("mti,mtj->tij", mine, others, precision=lax.Precision.HIGHEST) / (
            members - 1.0
        )
        offset = jnp.full((TPD,), shift - HALO_TILES).astype(jnp.float32)
        keep = lax.dynamic_index_in_dim(keep_table, shift, 1, keepdims=False)
        coefficient = taper(offset, TILE) * covar * keep[:, None, None]
        return total + jnp.einsum(
            "mtj,tij->mti", other_weights, coefficient, precision=lax.Precision.HIGHEST
        )

    total = lax.fori_loop(0, span_count, add_offset, jnp.zeros((members, TPD, TILE), jnp.float32))
    returned = lax.all_to_all(
        total.reshape(members, block), "member", split_axis=0, concat_axis=1, tiled=True
    )
    return returned


BLOCK = 2 * TILE
SPAN = HALO_TILES + 1
RIM = HALO_TILES * TILE


def split(value):
    high = value.astype(jnp.bfloat16)
    return high, (value - high.astype(jnp.float32)).astype(jnp.bfloat16)


def dot(left, right):
    return jnp.dot(left, right, preferred_element_type=jnp.float32)


def fill_taper(taper_ref, members):
    rows = lax.broadcasted_iota(jnp.int32, (BLOCK, BLOCK), 0)
    columns = lax.broadcasted_iota(jnp.int32, (BLOCK, BLOCK), 1)
    for k in range(SPAN):
        spread = (columns - rows + (2 * k - HALO_TILES) * TILE).astype(jnp.float32) / (2.0 * TILE)
        taper_ref[k] = 1.0 / ((1.0 + spread * spread) * (members - 1.0))


def prepare_states(value, block, own, low_ref, high_ref, low_t_ref, high_t_ref):
    anomaly = value - jnp.mean(value, axis=0, keepdims=True)
    high_ref[block], low_ref[block] = split(anomaly)
    if own is not None:
        high_t_ref[own], low_t_ref[own] = split(anomaly.T)


def prepare_weights(value, block, weight_ref):
    high = value.astype(jnp.bfloat16).astype(jnp.float32)
    weight_ref[block] = jnp.concatenate([high, value - high], axis=0).T.astype(jnp.bfloat16)


def pair_rows(pair, ks, keep_ref, low_ref, high_ref, low_t_ref, high_t_ref, taper_ref, x_high_ref, x_low_ref):
    for spot, k in enumerate(ks):
        left_high, left_low = high_t_ref[pair], low_t_ref[pair]
        right_high, right_low = high_ref[pair + k], low_ref[pair + k]
        covar = dot(left_high, right_high) + dot(left_low, right_high) + dot(left_high, right_low)
        scaled = covar * taper_ref[k]
        for s in range(2):
            for t in range(2):
                rows, columns = slice(s * TILE, (s + 1) * TILE), slice(t * TILE, (t + 1) * TILE)
                value = scaled[rows, columns] * keep_ref[2 * pair + s, 2 * k + t + 1 - s]
                place = slice((2 * spot + t) * TILE, (2 * spot + t + 1) * TILE)
                x_high_ref[rows, place], x_low_ref[rows, place] = split(value)


def pair_apply(pair, ks, weight_ref, x_high_ref, x_low_ref):
    depth = len(ks) * BLOCK
    weight = weight_ref[pl.ds(pair + ks[0], len(ks))].reshape(depth, weight_ref.shape[2])
    total = dot(x_high_ref[:, :depth], weight) + dot(x_low_ref[:, :depth], weight)
    half = total.shape[1] // 2
    return (total[:, :half] + total[:, half:]).T


def scratch_of(members, part, pairs):
    rim = RIM // BLOCK
    blocks = pairs + 2 * rim
    bf16 = jnp.bfloat16
    return [
        pltpu.VMEM((blocks, members, BLOCK), bf16),
        pltpu.VMEM((blocks, members, BLOCK), bf16),
        pltpu.VMEM((pairs, BLOCK, members), bf16),
        pltpu.VMEM((pairs, BLOCK, members), bf16),
        pltpu.VMEM((blocks, BLOCK, 2 * part), bf16),
        pltpu.VMEM((SPAN, BLOCK, BLOCK), jnp.float32),
    ] + [pltpu.VMEM((BLOCK, SPAN * BLOCK), bf16)] * 4


def keep_table_of(neighbours, factor_window, tiles_all):
    local_tiles = neighbours.shape[0]
    first = lax.axis_index("region") * local_tiles
    own = first + jnp.arange(local_tiles, dtype=jnp.int32)
    shift = (neighbours - own[:, None] + HALO_TILES + 1) % tiles_all
    places = jnp.arange(2 * SPAN + 2, dtype=jnp.int32)
    return jnp.sum((shift[:, :, None] == places).astype(jnp.float32), axis=1)


def region_kernel(
    own_ref, weights_ref, factor_ref, keep_ref, out_ref,
    low_ref, high_ref, low_t_ref, high_t_ref, weight_ref, taper_ref, xh0, xl0, xh1, xl1,
    held, weight_rim, factor_rim,
    direct_send, direct_recv, relay_send, relay_recv, rim_send, rim_recv,
):
    part, rows = own_ref.shape
    count = rows // RIM
    per_chunk = RIM // BLOCK
    half = part // 2
    member, region = lax.axis_index("member"), lax.axis_index("region")
    regions = lax.axis_size("region")
    beside = member + 1 - 2 * lax.rem(member, 2)
    across = lax.rem(member + 2, 4)
    partners = ((beside, region), (across, region))
    above = (member, lax.rem(region + 1, regions))
    below = (member, lax.rem(region + regions - 1, regions))

    barrier = pltpu.get_barrier_semaphore()
    for device in partners + (above, below):
        pl.semaphore_signal(barrier, inc=1, device_id=device, device_id_type=pl.DeviceIdType.MESH)
    pl.semaphore_wait(barrier, 4)

    def chunk_at(step):
        return step + 1

    def copy(source, target, send, recv, device):
        return pltpu.make_async_remote_copy(
            src_ref=source, dst_ref=target, send_sem=send, recv_sem=recv,
            device_id=device, device_id_type=pl.DeviceIdType.MESH,
        )

    def columns_of(chunk):
        return pl.ds(pl.multiple_of((chunk - 1) * RIM, RIM), RIM)

    def direct(step, side):
        chunk = chunk_at(step)
        return copy(
            own_ref.at[:, columns_of(chunk)], held.at[chunk, 1 + side],
            direct_send.at[side, step], direct_recv.at[side, step], partners[side],
        )

    def relay(step, side):
        chunk = chunk_at(step)
        strip = pl.ds(side * half, half)
        return copy(
            held.at[chunk, 2 - side, strip], held.at[chunk, 3, strip],
            relay_send.at[side, step], relay_recv.at[side, step], partners[side],
        )

    def rim(up, item):
        device = above if up else below
        edge, place = (count, 0) if up else (1, count + 1)
        spot = 0 if up else 1
        columns = slice((edge - 1) * RIM, edge * RIM)
        if item == 4:
            source, target = weights_ref.at[:, columns], weight_rim.at[spot]
        elif item == 5:
            source, target = factor_ref.at[:, columns], factor_rim.at[spot]
        elif item == 0:
            source, target = own_ref.at[:, columns], held.at[place, 0]
        else:
            source, target = held.at[edge, item], held.at[place, item]
        return copy(source, target, rim_send.at[spot, item], rim_recv.at[spot, item], device)

    for step in range(2):
        for side in range(2):
            direct(step, side).start()
    for item in (0, 4, 5):
        for up in (True, False):
            rim(up, item).start()

    fill_taper(taper_ref, part * 4)

    @pl.loop(0, count * per_chunk)
    def _(block):
        columns = pl.ds(pl.multiple_of(block * BLOCK, BLOCK), BLOCK)
        prepare_weights(weights_ref[:, columns] * factor_ref[0:1, columns], block + per_chunk, weight_ref)

    def prepare_own(chunk):
        @pl.loop(0, per_chunk)
        def _(b):
            block = (chunk - 1) * per_chunk + b
            inner = pl.ds(pl.multiple_of(b * BLOCK, BLOCK), BLOCK)
            mine = own_ref[:, pl.ds(pl.multiple_of(block * BLOCK, BLOCK), BLOCK)]
            value = jnp.concatenate([mine] + [held[chunk, slot, :, inner] for slot in range(1, 4)], axis=0)
            prepare_states(value, block + per_chunk, block, low_ref, high_ref, low_t_ref, high_t_ref)

    def prepare_rim(up):
        place, spot = (0, 0) if up else (count + 1, 1)

        @pl.loop(0, per_chunk)
        def _(b):
            inner = pl.ds(pl.multiple_of(b * BLOCK, BLOCK), BLOCK)
            value = jnp.concatenate([held[place, slot, :, inner] for slot in range(4)], axis=0)
            block = place * per_chunk + b
            prepare_states(value, block, None, low_ref, high_ref, low_t_ref, high_t_ref)
            prepare_weights(weight_rim[spot, :, inner] * factor_rim[spot, 0:1, inner], block, weight_ref)

    def work(group, first, last, fresh):
        buffers = ((xh0, xl0), (xh1, xl1))
        for start in range(0, per_chunk, 2):
            todo = []
            for p in (start, start + 1):
                ks = [k for k in range(SPAN) if first <= (k + p) // per_chunk <= last]
                todo.append((group * per_chunk + p, ks, buffers[p % 2]))
            for pair, ks, held_x in todo:
                pair_rows(pair, ks, keep_ref, low_ref, high_ref, low_t_ref, high_t_ref, taper_ref, *held_x)
            for pair, ks, held_x in todo:
                columns = pl.ds(pl.multiple_of(pair * BLOCK, BLOCK), BLOCK)
                term = pair_apply(pair, ks, weight_ref, *held_x)
                out_ref[:, columns] = term if fresh else out_ref[:, columns] + term

    @pl.loop(0, count + 2)
    def _(step):
        @pl.when(step < count)
        def _():
            for side in range(2):
                direct(step, side).wait_recv()
            for side in range(2):
                relay(step, side).start()

        @pl.when(step + 2 < count)
        def _():
            for side in range(2):
                direct(step + 2, side).start()

        for first, up in ((0, False), (count - 1, True)):
            @pl.when(step == first)
            def _():
                for item in (1, 2):
                    rim(up, item).start()

        @pl.when((step >= 1) & (step <= count))
        def _():
            for side in range(2):
                relay(step - 1, side).wait_recv()

        for first, up in ((1, False), (count, True)):
            @pl.when(step == first)
            def _():
                rim(up, 3).start()

        @pl.when((step >= 1) & (step <= count))
        def _():
            prepare_own(chunk_at(step - 1))

        @pl.when(step == 1)
        def _():
            work(0, 1, 1, True)

        @pl.when((step >= 2) & (step <= count))
        def _():
            work(step - 1, 0, 1, True)

        @pl.when(step == count + 1)
        def _():
            for item in range(6):
                rim(False, item).wait_recv()
            prepare_rim(False)

        @pl.when(step >= 2)
        def _():
            work(step - 2, 2, 2, False)

    for item in range(6):
        rim(True, item).wait_recv()
    prepare_rim(True)
    work(0, 0, 0, False)

    @pl.loop(0, count)
    def _(step):
        for side in range(2):
            direct(step, side).wait_send()
            relay(step, side).wait_send()

    for up in (True, False):
        for item in range(6):
            rim(up, item).wait_send()


def region_shards(states, weights, obs_count, neighbours):
    region_count = lax.axis_size("region")
    part, local_rows = states.shape
    members = part * lax.axis_size("member")
    count = local_rows // RIM
    pairs = local_rows // BLOCK
    counts = obs_count.astype(jnp.float32)
    factor = counts / (counts + 8.0)
    factor_rows = jnp.broadcast_to(factor[None, :, None], (8, local_rows // TILE, TILE)).reshape(8, local_rows)
    keep = keep_table_of(neighbours, None, region_count * (local_rows // TILE))
    vmem = pl.BlockSpec(memory_space=pltpu.VMEM)
    dma = pltpu.SemaphoreType.DMA
    return pl.pallas_call(
        region_kernel,
        out_shape=jax.ShapeDtypeStruct((part, local_rows), jnp.float32),
        in_specs=[vmem, vmem, vmem, pl.BlockSpec(memory_space=pltpu.SMEM)],
        out_specs=vmem,
        scratch_shapes=scratch_of(members, part, pairs)
        + [
            pltpu.VMEM((count + 2, 4, part, RIM), jnp.float32),
            pltpu.VMEM((2, part, RIM), jnp.float32),
            pltpu.VMEM((2, 8, RIM), jnp.float32),
            dma((2, count)), dma((2, count)), dma((2, count)), dma((2, count)),
            dma((2, 6)), dma((2, 6)),
        ],
        compiler_params=pltpu.CompilerParams(
            collective_id=0, has_side_effects=True, vmem_limit_bytes=60 * 1024 * 1024
        ),
    )(states, weights, factor_rows, keep)


def fits(states, weights, obs_count, neighbours):
    part, local_rows = states.shape
    members = part * lax.axis_size("member")
    window = local_rows + 2 * RIM
    return (
        lax.axis_size("member") == 4
        and lax.axis_size("region") > 2
        and local_rows % RIM == 0
        and local_rows >= 3 * RIM
        and members % 128 == 0
        and part % 64 == 0
        and window * (members * 12 + part * 16) <= 46 * 1024 * 1024
    )


def either(*arguments):
    return region_shards(*arguments) if fits(*arguments) else shards(*arguments)


def solution(mesh):
    placed = (P("member", "region"), P("member", "region"), P("region"), P("region", None))
    return jax.shard_map(
        either, mesh=mesh, in_specs=placed, out_specs=P("member", "region"), check_vma=False
    )
```

```python
import jax
import jax.numpy as jnp
from jax import lax
from jax.experimental import pallas as pl
from jax.experimental.pallas import tpu as pltpu
from jax.sharding import PartitionSpec as P

TILE = 128
HALO_TILES = 8
TPD = 12


def extended_2(block, sides, width):
    for axis, dim in sides:
        count = lax.axis_size(axis)
        forward = [(i, i + 1) for i in range(count - 1)]
        forward.append((count - 1, 0))
        backward = [(target, source) for source, target in forward]
        low = lax.ppermute(
            lax.slice_in_dim(block, block.shape[dim] - width, None, axis=dim), axis, forward
        )
        high = lax.ppermute(lax.slice_in_dim(block, 0, width, axis=dim), axis, backward)
        block = jnp.concatenate([low, block, high], axis=dim)
    return block


def taper(offset, tile):
    rows = jnp.arange(tile, dtype=jnp.float32)
    spread = tile * offset[:, None, None] + rows[None, None, :] - rows[None, :, None]
    scaled = spread / (2.0 * tile)
    return 1.0 / (1.0 + scaled * scaled)


def shards(states, weights, obs_count, neighbours):
    member_count = lax.axis_size("member")
    region_count = lax.axis_size("region")
    member_part, local_rows = states.shape
    local_tiles = local_rows // TILE
    counts = obs_count.astype(jnp.float32)
    factor = counts / (counts + 8.0)
    scaled = (weights.reshape(member_part, local_tiles, TILE) * factor[None, :, None]).reshape(
        member_part, local_rows
    )
    stacked = jnp.stack([states, scaled])
    rim = HALO_TILES * TILE
    block = TPD * TILE
    padded = extended_2(stacked, (("region", 2),), rim)
    own_block = lax.all_to_all(stacked, "member", split_axis=2, concat_axis=1, tiled=True)
    extended = extended_2(own_block, (("member", 2),), rim)
    below, above = (
        lax.all_gather(padded[:, :, :rim], "member", axis=1, tiled=True),
        lax.all_gather(padded[:, :, rim + local_rows :], "member", axis=1, tiled=True),
    )
    position = lax.axis_index("member")
    lower = jnp.where(position == 0, below, extended[:, :, :rim])
    upper = jnp.where(position == member_count - 1, above, extended[:, :, rim + block :])
    window = jnp.concatenate([lower, extended[:, :, rim : rim + block], upper], axis=2)
    members = window.shape[1]
    anomaly = window[0] - jnp.mean(window[0], axis=0, keepdims=True)
    window_weights = window[1]
    tiles_all = TPD * member_count * region_count
    first_tile = (lax.axis_index("region") * member_count + lax.axis_index("member")) * TPD
    lists = lax.dynamic_slice_in_dim(neighbours, lax.axis_index("member") * TPD, TPD, 0)
    local_ids = (lists - first_tile + HALO_TILES) % tiles_all
    span_count = 2 * HALO_TILES + 1
    tile_places = jnp.arange(TPD, dtype=jnp.int32)
    shift_places = jnp.arange(span_count, dtype=jnp.int32)
    wanted = tile_places[:, None, None] + shift_places[None, None, :]
    keep_table = jnp.sum((local_ids[:, :, None] == wanted).astype(jnp.float32), axis=1)
    mine = anomaly[:, rim : rim + block].reshape(members, TPD, TILE)

    def add_offset(shift, total):
        others = lax.dynamic_slice_in_dim(anomaly, shift * TILE, block, 1).reshape(
            members, TPD, TILE
        )
        other_weights = lax.dynamic_slice_in_dim(window_weights, shift * TILE, block, 1).reshape(
            members, TPD, TILE
        )
        covar = jnp.einsum("mti,mtj->tij", mine, others, precision=lax.Precision.HIGHEST) / (
            members - 1.0
        )
        offset = jnp.full((TPD,), shift - HALO_TILES).astype(jnp.float32)
        keep = lax.dynamic_index_in_dim(keep_table, shift, 1, keepdims=False)
        coefficient = taper(offset, TILE) * covar * keep[:, None, None]
        return total + jnp.einsum(
            "mtj,tij->mti", other_weights, coefficient, precision=lax.Precision.HIGHEST
        )

    total = lax.fori_loop(0, span_count, add_offset, jnp.zeros((members, TPD, TILE), jnp.float32))
    returned = lax.all_to_all(
        total.reshape(members, block), "member", split_axis=0, concat_axis=1, tiled=True
    )
    return returned


BLOCK = 2 * TILE
SPAN = HALO_TILES + 1
RIM = HALO_TILES * TILE


def split(value):
    high = value.astype(jnp.bfloat16)
    return high, (value - high.astype(jnp.float32)).astype(jnp.bfloat16)


def dot(left, right):
    return jnp.dot(left, right, preferred_element_type=jnp.float32)


def fill_taper(taper_ref, members):
    rows = lax.broadcasted_iota(jnp.int32, (BLOCK, BLOCK), 0)
    columns = lax.broadcasted_iota(jnp.int32, (BLOCK, BLOCK), 1)
    for k in range(SPAN):
        spread = (columns - rows + (2 * k - HALO_TILES) * TILE).astype(jnp.float32) / (2.0 * TILE)
        taper_ref[k] = 1.0 / ((1.0 + spread * spread) * (members - 1.0))


def prepare_states(value, block, own, low_ref, high_ref, low_t_ref, high_t_ref):
    anomaly = value - jnp.mean(value, axis=0, keepdims=True)
    high_ref[block], low_ref[block] = split(anomaly)
    if own is not None:
        high_t_ref[own], low_t_ref[own] = split(anomaly.T)


def prepare_weights(value, block, weight_ref):
    high = value.astype(jnp.bfloat16).astype(jnp.float32)
    weight_ref[block] = jnp.concatenate([high, value - high], axis=0).T.astype(jnp.bfloat16)


def pair_rows(pair, ks, keep_ref, low_ref, high_ref, low_t_ref, high_t_ref, taper_ref, x_high_ref, x_low_ref):
    for spot, k in enumerate(ks):
        left_high, left_low = high_t_ref[pair], low_t_ref[pair]
        right_high, right_low = high_ref[pair + k], low_ref[pair + k]
        covar = dot(left_high, right_high) + dot(left_low, right_high) + dot(left_high, right_low)
        scaled = covar * taper_ref[k]
        for s in range(2):
            for t in range(2):
                rows, columns = slice(s * TILE, (s + 1) * TILE), slice(t * TILE, (t + 1) * TILE)
                value = scaled[rows, columns] * keep_ref[2 * pair + s, 2 * k + t + 1 - s]
                place = slice((2 * spot + t) * TILE, (2 * spot + t + 1) * TILE)
                x_high_ref[rows, place], x_low_ref[rows, place] = split(value)


def pair_apply(pair, ks, weight_ref, x_high_ref, x_low_ref):
    depth = len(ks) * BLOCK
    weight = weight_ref[pl.ds(pair + ks[0], len(ks))].reshape(depth, weight_ref.shape[2])
    total = dot(x_high_ref[:, :depth], weight) + dot(x_low_ref[:, :depth], weight)
    half = total.shape[1] // 2
    return (total[:, :half] + total[:, half:]).T


def scratch_of(members, part, pairs):
    rim = RIM // BLOCK
    blocks = pairs + 2 * rim
    bf16 = jnp.bfloat16
    return [
        pltpu.VMEM((blocks, members, BLOCK), bf16),
        pltpu.VMEM((blocks, members, BLOCK), bf16),
        pltpu.VMEM((pairs, BLOCK, members), bf16),
        pltpu.VMEM((pairs, BLOCK, members), bf16),
        pltpu.VMEM((blocks, BLOCK, 2 * part), bf16),
        pltpu.VMEM((SPAN, BLOCK, BLOCK), jnp.float32),
    ] + [pltpu.VMEM((BLOCK, SPAN * BLOCK), bf16)] * 4


def keep_table_of(neighbours, factor_window, tiles_all):
    local_tiles = neighbours.shape[0]
    first = lax.axis_index("region") * local_tiles
    own = first + jnp.arange(local_tiles, dtype=jnp.int32)
    shift = (neighbours - own[:, None] + HALO_TILES + 1) % tiles_all
    places = jnp.arange(2 * SPAN + 2, dtype=jnp.int32)
    return jnp.sum((shift[:, :, None] == places).astype(jnp.float32), axis=1)


def region_kernel(
    own_ref, weights_ref, factor_ref, keep_ref, out_ref,
    low_ref, high_ref, low_t_ref, high_t_ref, weight_ref, taper_ref, xh0, xl0, xh1, xl1,
    held, weight_rim, factor_rim,
    direct_send, direct_recv, relay_send, relay_recv, rim_send, rim_recv,
):
    part, rows = own_ref.shape
    count = rows // RIM
    per_chunk = RIM // BLOCK
    half = part // 2
    member, region = lax.axis_index("member"), lax.axis_index("region")
    regions = lax.axis_size("region")
    beside = member + 1 - 2 * lax.rem(member, 2)
    across = lax.rem(member + 2, 4)
    partners = ((beside, region), (across, region))
    above = (member, lax.rem(region + 1, regions))
    below = (member, lax.rem(region + regions - 1, regions))

    barrier = pltpu.get_barrier_semaphore()
    for device in partners + (above, below):
        pl.semaphore_signal(barrier, inc=1, device_id=device, device_id_type=pl.DeviceIdType.MESH)
    pl.semaphore_wait(barrier, 4)

    def chunk_at(step):
        return step + 1

    def copy(source, target, send, recv, device):
        return pltpu.make_async_remote_copy(
            src_ref=source, dst_ref=target, send_sem=send, recv_sem=recv,
            device_id=device, device_id_type=pl.DeviceIdType.MESH,
        )

    def columns_of(chunk):
        return pl.ds(pl.multiple_of((chunk - 1) * RIM, RIM), RIM)

    def direct(step, side):
        chunk = chunk_at(step)
        return copy(
            own_ref.at[:, columns_of(chunk)], held.at[chunk, 1 + side],
            direct_send.at[side, step], direct_recv.at[side, step], partners[side],
        )

    def relay(step, side):
        chunk = chunk_at(step)
        strip = pl.ds(side * half, half)
        return copy(
            held.at[chunk, 2 - side, strip], held.at[chunk, 3, strip],
            relay_send.at[side, step], relay_recv.at[side, step], partners[side],
        )

    def rim(up, item):
        device = above if up else below
        edge, place = (count, 0) if up else (1, count + 1)
        spot = 0 if up else 1
        columns = slice((edge - 1) * RIM, edge * RIM)
        if item == 4:
            source, target = weights_ref.at[:, columns], weight_rim.at[spot]
        elif item == 5:
            source, target = factor_ref.at[:, columns], factor_rim.at[spot]
        elif item == 0:
            source, target = own_ref.at[:, columns], held.at[place, 0]
        else:
            source, target = held.at[edge, item], held.at[place, item]
        return copy(source, target, rim_send.at[spot, item], rim_recv.at[spot, item], device)

    for step in range(2):
        for side in range(2):
            direct(step, side).start()
    for item in (0, 4, 5):
        for up in (True, False):
            rim(up, item).start()

    fill_taper(taper_ref, part * 4)

    @pl.loop(0, count * per_chunk)
    def _(block):
        columns = pl.ds(pl.multiple_of(block * BLOCK, BLOCK), BLOCK)
        prepare_weights(weights_ref[:, columns] * factor_ref[0:1, columns], block + per_chunk, weight_ref)

    def prepare_own(chunk):
        @pl.loop(0, per_chunk)
        def _(b):
            block = (chunk - 1) * per_chunk + b
            inner = pl.ds(pl.multiple_of(b * BLOCK, BLOCK), BLOCK)
            mine = own_ref[:, pl.ds(pl.multiple_of(block * BLOCK, BLOCK), BLOCK)]
            value = jnp.concatenate([mine] + [held[chunk, slot, :, inner] for slot in range(1, 4)], axis=0)
            prepare_states(value, block + per_chunk, block, low_ref, high_ref, low_t_ref, high_t_ref)

    def prepare_rim(up):
        place, spot = (0, 0) if up else (count + 1, 1)

        @pl.loop(0, per_chunk)
        def _(b):
            inner = pl.ds(pl.multiple_of(b * BLOCK, BLOCK), BLOCK)
            value = jnp.concatenate([held[place, slot, :, inner] for slot in range(4)], axis=0)
            block = place * per_chunk + b
            prepare_states(value, block, None, low_ref, high_ref, low_t_ref, high_t_ref)
            prepare_weights(weight_rim[spot, :, inner] * factor_rim[spot, 0:1, inner], block, weight_ref)

    def work(group, first, last, fresh):
        buffers = ((xh0, xl0), (xh1, xl1))
        for start in range(0, per_chunk, 2):
            todo = []
            for p in (start, start + 1):
                ks = [k for k in range(SPAN) if first <= (k + p) // per_chunk <= last]
                todo.append((group * per_chunk + p, ks, buffers[p % 2]))
            for pair, ks, held_x in todo:
                pair_rows(pair, ks, keep_ref, low_ref, high_ref, low_t_ref, high_t_ref, taper_ref, *held_x)
            for pair, ks, held_x in todo:
                columns = pl.ds(pl.multiple_of(pair * BLOCK, BLOCK), BLOCK)
                term = pair_apply(pair, ks, weight_ref, *held_x)
                out_ref[:, columns] = term if fresh else out_ref[:, columns] + term

    @pl.loop(0, count + 2)
    def _(step):
        @pl.when(step < count)
        def _():
            for side in range(2):
                direct(step, side).wait_recv()
            for side in range(2):
                relay(step, side).start()

        @pl.when(step + 2 < count)
        def _():
            for side in range(2):
                direct(step + 2, side).start()

        for first, up in ((0, False), (count - 1, True)):
            @pl.when(step == first)
            def _():
                for item in (1, 2):
                    rim(up, item).start()

        @pl.when((step >= 1) & (step <= count))
        def _():
            for side in range(2):
                relay(step - 1, side).wait_recv()

        for first, up in ((1, False), (count, True)):
            @pl.when(step == first)
            def _():
                rim(up, 3).start()

        @pl.when((step >= 1) & (step <= count))
        def _():
            prepare_own(chunk_at(step - 1))

        @pl.when(step == 1)
        def _():
            work(0, 1, 1, True)

        @pl.when((step >= 2) & (step <= count))
        def _():
            work(step - 1, 0, 1, True)

        @pl.when(step == count + 1)
        def _():
            for item in range(6):
                rim(False, item).wait_recv()
            prepare_rim(False)

        @pl.when(step >= 2)
        def _():
            work(step - 2, 2, 2, False)

    for item in range(6):
        rim(True, item).wait_recv()
    prepare_rim(True)
    work(0, 0, 0, False)

    @pl.loop(0, count)
    def _(step):
        for side in range(2):
            direct(step, side).wait_send()
            relay(step, side).wait_send()

    for up in (True, False):
        for item in range(6):
            rim(up, item).wait_send()


def region_shards(states, weights, obs_count, neighbours):
    region_count = lax.axis_size("region")
    part, local_rows = states.shape
    members = part * lax.axis_size("member")
    count = local_rows // RIM
    pairs = local_rows // BLOCK
    counts = obs_count.astype(jnp.float32)
    factor = counts / (counts + 8.0)
    factor_rows = jnp.broadcast_to(factor[None, :, None], (8, local_rows // TILE, TILE)).reshape(8, local_rows)
    keep = keep_table_of(neighbours, None, region_count * (local_rows // TILE))
    vmem = pl.BlockSpec(memory_space=pltpu.VMEM)
    dma = pltpu.SemaphoreType.DMA
    return pl.pallas_call(
        region_kernel,
        out_shape=jax.ShapeDtypeStruct((part, local_rows), jnp.float32),
        in_specs=[vmem, vmem, vmem, pl.BlockSpec(memory_space=pltpu.SMEM)],
        out_specs=vmem,
        scratch_shapes=scratch_of(members, part, pairs)
        + [
            pltpu.VMEM((count + 2, 4, part, RIM), jnp.float32),
            pltpu.VMEM((2, part, RIM), jnp.float32),
            pltpu.VMEM((2, 8, RIM), jnp.float32),
            dma((2, count)), dma((2, count)), dma((2, count)), dma((2, count)),
            dma((2, 6)), dma((2, 6)),
        ],
        compiler_params=pltpu.CompilerParams(
            collective_id=0, has_side_effects=True, vmem_limit_bytes=42 * 1024 * 1024
        ),
    )(states, weights, factor_rows, keep)


def fits(states, weights, obs_count, neighbours):
    part, local_rows = states.shape
    members = part * lax.axis_size("member")
    window = local_rows + 2 * RIM
    return (
        lax.axis_size("member") == 4
        and lax.axis_size("region") > 2
        and local_rows % RIM == 0
        and local_rows >= 3 * RIM
        and members % 128 == 0
        and part % 64 == 0
        and window * (members * 12 + part * 16) <= 46 * 1024 * 1024
    )


def either(*arguments):
    return region_shards(*arguments) if fits(*arguments) else shards(*arguments)


def solution(mesh):
    placed = (P("member", "region"), P("member", "region"), P("region"), P("region", None))
    return jax.shard_map(
        either, mesh=mesh, in_specs=placed, out_specs=P("member", "region"), check_vma=False
    )
```
